32 devices in a mesh: ex: 8 (over z, x), feat: 4 (over y, core).
Axes of the slice: x: 2, y: 2, z: 4, core: 2. Of those that a mesh axis runs over, the one named last changes fastest.
Arguments:
- train_grads: bfloat16 [3072, 16384], P('ex', 'feat'), may hold values from -6 to 6
- projection: bfloat16 [16384, 4096], P('feat', 'ex'), may hold values from -0.046875 to 0.046875
- test_features: bfloat16 [256, 4096], P('ex', 'feat'), may hold values from -0.09375 to 0.09375
- example_weights: float32 [3072], P('ex'), may hold values from 0.05 to 1
Outputs:
- scores: float32 [256, 3072], P('feat', 'ex')
- projected: bfloat16 [3072, 4096], P('ex', 'feat')
The draws below stay inside these ranges and needn't reach their ends.
All inputs are finite; a program needn't handle non-finite values.
Results may differ from the reference program's by a relative error of at most 0.0031.
Values may be sent and summed in bfloat16 or wider, within the bound.
No kernel may reach another device: no remote copies, remote signals or barrier semaphores. Data moves between devices by JAX's collectives and lax.ppermute only.
A program may use at most 192 MiB of HBM per device.

```python
import math
import jax
import jax.numpy as jnp
from jax import lax

P_SIZE = 16384
K = 4096
NTR = 3072
NTE = 256


def levels(own_key, shape, split, least, top_value):
    gain = 1.0
    for dim, blocks in split:
        draws = jax.random.uniform(jax.random.fold_in(jax.random.fold_in(own_key, 6), dim), (blocks,), jnp.float32, least / len(split), top_value / len(split))
        gain = gain * jnp.repeat(jnp.exp(draws), shape[dim] // blocks).reshape((-1,) + (1,) * (len(shape) - 1 - dim))
    return gain


def gaussian(key, extent, deviation, reach, cuts=(), kind=jnp.bfloat16):
    entries = deviation * jax.random.normal(key, extent, jnp.float32)
    if cuts:
        entries = entries * levels(key, extent, cuts, -0.22, 0.18)
    return jnp.clip(entries, -reach, reach).astype(kind)


def setup_inputs(seed: int = 0) -> dict:
    splits = jax.random.split(jax.random.key(seed), 5)
    train_grads = gaussian(splits[0], (NTR, P_SIZE), 1.0, 6.0, ((0, 8), (1, 4)))
    projection = gaussian(splits[1], (P_SIZE, K), P_SIZE ** -0.5, 0.046875, ((0, 4), (1, 8)))
    test_features = gaussian(splits[2], (NTE, K), K ** -0.5, 0.09375, ((0, 8), (1, 4)))
    example_weights = jnp.clip(jnp.exp(math.log(1.0) - 2.9957323 * jax.random.uniform(splits[3], (NTR,), jnp.float32) ** levels(splits[3], (NTR,), ((0, 8),), -0.2, 0.2)), 0.05, 1.0)
    return dict(train_grads=train_grads, projection=projection, test_features=test_features, example_weights=example_weights)


def reference(train_grads, projection, test_features, example_weights):
    projected = jnp.dot(train_grads, projection, preferred_element_type=jnp.float32).astype(jnp.bfloat16)
    inner = lax.dot_general(test_features, projected, (((1,), (1,)), ((), ())), preferred_element_type=jnp.float32)
    return inner * example_weights[None, :], projected
```

```python
import jax
import jax.numpy as jnp
from jax import lax
from jax.sharding import PartitionSpec as P


def solution(mesh):
    E, F = mesh.shape["ex"], mesh.shape["feat"]
    L = 2
    H = F // L
    X = E // F
    both = ("ex", "feat")

    def ex_of(h, l, x):
        return (h * L + l) * X + x

    coords = [(h, l, x) for h in range(H) for l in range(L) for x in range(X)]

    def shift_h(d):
        return [(ex_of(h, l, x), ex_of((h + d) % H, l, x)) for h, l, x in coords]

    def shift_l(d):
        return [(ex_of(h, l, x), ex_of(h, (l + d) % L, x)) for h, l, x in coords]

    def shift_x(d):
        return [(ex_of(h, l, x), ex_of(h, l, (x + d) % X)) for h, l, x in coords]

    def shift_c(d):
        return [(y * L + c, y * L + (c + d) % L) for y in range(H) for c in range(L)]

    def shift_y(d):
        return [(y * L + c, (y + d) % H * L + c) for y in range(H) for c in range(L)]

    def home(d):
        return [
            (ex_of(h, l, x) * F + y * L + c, ex_of(y, l, (x - d) % X) * F + h * L + c)
            for h, l, x in coords
            for y in range(H)
            for c in range(L)
        ]

    def pick(options, index):
        out = options[0]
        for i in range(1, len(options)):
            out = jnp.where(index == i, options[i], out)
        return out

    def dot(a, b):
        return jnp.dot(a, b, preferred_element_type=jnp.float32)

    def local(a, b, test, weights):
        rows, cols = a.shape[0], b.shape[1]
        e, f = lax.axis_index("ex"), lax.axis_index("feat")
        h, l, x = e // (L * X), e // X % L, e % X
        y, c = f // L, f % L
        n_a, n_b = 3, 4 if cols % 512 == 0 else 1
        ra, cb = rows // n_a, cols // n_b

        a_parts = [a[i * ra : (i + 1) * ra] for i in range(n_a)]
        b_parts = [b[:, j * cb : (j + 1) * cb] for j in range(n_b)]
        sets = []
        for dh in range(H):
            first = a_parts if dh == 0 else [lax.ppermute(p, "ex", shift_h(dh)) for p in a_parts]
            if dh == 0:
                first_x = [[lax.ppermute(a, "ex", shift_x(dx))] for dx in range(1, X)]
                sets.append([[a]] + first_x)
            else:
                sets.append(
                    [first]
                    + [[lax.ppermute(p, "ex", shift_x(dx)) for p in first] for dx in range(1, X)]
                )
        b_sets = [b_parts] + [
            [lax.ppermute(p, "ex", shift_l(dl)) for p in b_parts] for dl in range(1, L)
        ]
        tests = lax.all_gather(test, "ex", axis=0, tiled=True)

        got = [[] for _ in range(X)]
        for j in range(n_b):
            summed = []
            prods = [
                [
                    jnp.concatenate(
                        [dot(p, b_sets[dl][j]) for s in sets[dh] for p in s], axis=0
                    )
                    for dh in range(H)
                ]
                for dl in range(L)
            ]
            mine = []
            for dh in range(H):
                blocks = [prods[dl][dh] for dl in range(L)]
                total = pick(blocks, (l - c) % L)
                for d in range(1, L):
                    total = total + lax.ppermute(
                        pick(blocks, (l - c - d) % L), "feat", shift_c(d)
                    )
                mine.append(total)
            total = pick(mine, (h - y) % H)
            for d in range(1, H):
                total = total + lax.ppermute(
                    pick(mine, (h - y - d) % H).astype(jnp.bfloat16), "feat", shift_y(d)
                ).astype(jnp.float32)
            final = total.astype(jnp.bfloat16)
            for dx in range(X):
                got[dx].append(
                    lax.ppermute(final[dx * rows : (dx + 1) * rows], both, home(dx))
                )
        blocks = [jnp.concatenate(g, axis=1) for g in got]
        projected = jnp.concatenate(
            [pick(blocks, (k - x) % X) for k in range(X)], axis=1
        )

        part = lax.dot_general(
            tests, projected, (((1,), (1,)), ((), ())), preferred_element_type=jnp.float32
        )
        half = part.shape[0] // F
        part = part.reshape(H, L, half, part.shape[1])
        mine = lax.dynamic_index_in_dim(part, c, 1, keepdims=False)
        for d in range(1, L):
            mine = mine + lax.ppermute(
                lax.dynamic_index_in_dim(part, (c + d) % L, 1, keepdims=False), "feat", shift_c(d)
            )
        inner = lax.dynamic_index_in_dim(mine, y, 0, keepdims=False)
        for d in range(1, H):
            inner = inner + lax.ppermute(
                lax.dynamic_index_in_dim(mine, (y + d) % H, 0, keepdims=False), "feat", shift_y(d)
            )
        return inner * weights[None, :], projected

    return jax.shard_map(
        local,
        mesh=mesh,
        in_specs=(P("ex", "feat"), P("feat", "ex"), P("ex", "feat"), P("ex")),
        out_specs=(P("feat", "ex"), P("ex", "feat")),
        check_vma=False,
    )
```

```python
import jax
import jax.numpy as jnp
from jax import lax
from jax.sharding import PartitionSpec as P


def solution(mesh):
    E, F = mesh.shape["ex"], mesh.shape["feat"]
    L = 2
    H = F // L
    X = E // F
    both = ("ex", "feat")

    def ex_of(h, l, x):
        return (h * L + l) * X + x

    coords = [(h, l, x) for h in range(H) for l in range(L) for x in range(X)]

    def shift_h(d):
        return [(ex_of(h, l, x), ex_of((h + d) % H, l, x)) for h, l, x in coords]

    def shift_l(d):
        return [(ex_of(h, l, x), ex_of(h, (l + d) % L, x)) for h, l, x in coords]

    def shift_x(d):
        return [(ex_of(h, l, x), ex_of(h, l, (x + d) % X)) for h, l, x in coords]

    def shift_c(d):
        return [(y * L + c, y * L + (c + d) % L) for y in range(H) for c in range(L)]

    def shift_y(d):
        return [(y * L + c, (y + d) % H * L + c) for y in range(H) for c in range(L)]

    def home(d):
        return [
            (ex_of(h, l, x) * F + y * L + c, ex_of(y, l, (x - d) % X) * F + h * L + c)
            for h, l, x in coords
            for y in range(H)
            for c in range(L)
        ]

    def pick(options, index):
        out = options[0]
        for i in range(1, len(options)):
            out = jnp.where(index == i, options[i], out)
        return out

    def dot(a, b):
        return jnp.dot(a, b, preferred_element_type=jnp.float32)

    def local(a, b, test, weights):
        rows, cols = a.shape[0], b.shape[1]
        e, f = lax.axis_index("ex"), lax.axis_index("feat")
        h, l, x = e // (L * X), e // X % L, e % X
        y, c = f // L, f % L
        r_cuts = [0, rows - rows // 3, rows]
        c_cuts = [0, cols // 2, cols // 4 * 3, cols] if cols % 512 == 0 else [0, cols]
        n_r, n_c = len(r_cuts) - 1, len(c_cuts) - 1

        a_in = [a[r_cuts[i] : r_cuts[i + 1]] for i in range(n_r)]
        b_in = [b[:, c_cuts[j] : c_cuts[j + 1]] for j in range(n_c)]
        a_h = [[lax.ppermute(p, "ex", shift_h(dh)) for p in a_in] for dh in range(1, H)]
        b_l = [[lax.ppermute(p, "ex", shift_l(dl)) for p in b_in] for dl in range(1, L)]
        a_x = [lax.ppermute(a, "ex", shift_x(dx)) for dx in range(1, X)]
        sets = [[a_in] + [[v[r_cuts[i] : r_cuts[i + 1]] for i in range(n_r)] for v in a_x]]
        for pieces in a_h:
            sets.append(
                [pieces]
                + [[lax.ppermute(p, "ex", shift_x(dx)) for p in pieces] for dx in range(1, X)]
            )
        b_sets = [b_in] + b_l
        b_for = [
            [pick([b_sets[dl][j] for dl in range(L)], (l - c - d) % L) for j in range(n_c)]
            for d in range(L)
        ]

        late, _ = lax.optimization_barrier((test, a_h[-1][-1] if a_h else test))
        tests = late
        for axis_shift, n in ((shift_h, H), (shift_l, L), (shift_x, X)):
            tests = jnp.stack(
                [tests] + [lax.ppermute(tests, "ex", axis_shift(d)) for d in range(1, n)]
            )
        tests = jnp.transpose(tests, (2, 1, 0, 3, 4))
        tests = tests.reshape(-1, tests.shape[-1])

        def unit(parts, groups):
            def product(d, dh):
                return jnp.concatenate(
                    [
                        jnp.concatenate([dot(sets[dh][dx][i], b_for[d][j]) for j in groups], axis=1)
                        for dx in range(X)
                        for i in parts
                    ],
                    axis=0,
                )

            sent = [
                [lax.ppermute(product(d, dh), "feat", shift_c(d)) for dh in range(H)]
                for d in range(1, L)
            ]
            sums = []
            for dh in range(H):
                total = product(0, dh)
                for s in sent:
                    total = total + s[dh]
                sums.append(total)
            total = pick(sums, (h - y) % H)
            for d in range(1, H):
                out = pick(sums, (h - y - d) % H).astype(jnp.bfloat16)
                total = total + lax.ppermute(out, "feat", shift_y(d)).astype(jnp.float32)
            final = total.astype(jnp.bfloat16)
            n = final.shape[0] // X
            return [lax.ppermute(final[dx * n : (dx + 1) * n], both, home(dx)) for dx in range(X)]

        every = list(range(n_r))
        got = {}

        def store(parts, groups):
            res = unit(parts, groups)
            for dx in range(X):
                r = 0
                for i in parts:
                    k = 0
                    for j in groups:
                        nr, nc = r_cuts[i + 1] - r_cuts[i], c_cuts[j + 1] - c_cuts[j]
                        got[dx, i, j] = res[dx][r : r + nr, k : k + nc]
                        k += nc
                    r += nr

        for j in range(n_c - 1):
            store(every[:-1], [j])
        if n_c > 1:
            store(every[-1:], list(range(n_c - 1)))
        store(every, [n_c - 1])

        blocks = [
            jnp.concatenate(
                [
                    jnp.concatenate([got[dx, i, j] for j in range(n_c)], axis=1)
                    for i in range(n_r)
                ],
                axis=0,
            )
            for dx in range(X)
        ]
        projected = jnp.concatenate([pick(blocks, (k - x) % X) for k in range(X)], axis=1)

        part = lax.dot_general(
            tests, projected, (((1,), (1,)), ((), ())), preferred_element_type=jnp.float32
        )
        part = part.reshape(H, L, part.shape[0] // F, part.shape[1])
        mine = lax.dynamic_index_in_dim(part, (l - c) % L, 1, keepdims=False)
        for d in range(1, L):
            mine = mine + lax.ppermute(
                lax.dynamic_index_in_dim(part, (l - c - d) % L, 1, keepdims=False),
                "feat",
                shift_c(d),
            )
        inner = lax.dynamic_index_in_dim(mine, (h - y) % H, 0, keepdims=False)
        for d in range(1, H):
            inner = inner + lax.ppermute(
                lax.dynamic_index_in_dim(mine, (h - y - d) % H, 0, keepdims=False),
                "feat",
                shift_y(d),
            )
        own = inner.shape[0] // X
        inner = jnp.concatenate(
            [
                pick([inner[d * own : (d + 1) * own] for d in range(X)], (x - k) % X)
                for k in range(X)
            ],
            axis=0,
        )
        return inner * weights[None, :], projected

    return jax.shard_map(
        local,
        mesh=mesh,
        in_specs=(P("ex", "feat"), P("feat", "ex"), P("ex", "feat"), P("ex")),
        out_specs=(P("feat", "ex"), P("ex", "feat")),
        check_vma=False,
    )
```

```python
import jax
import jax.numpy as jnp
from jax import lax
from jax.sharding import PartitionSpec as P


def solution(mesh):
    E, F = mesh.shape["ex"], mesh.shape["feat"]
    L = 2
    H = F // L
    X = E // F
    Q = X // H
    both = ("ex", "feat")

    def ex_of(h, l, x):
        return (h * L + l) * X + x

    coords = [(h, l, x) for h in range(H) for l in range(L) for x in range(X)]

    def shift_h(d):
        return [(ex_of(h, l, x), ex_of((h + d) % H, l, x)) for h, l, x in coords]

    def shift_l(d):
        return [(ex_of(h, l, x), ex_of(h, (l + d) % L, x)) for h, l, x in coords]

    def shift_x(d):
        return [(ex_of(h, l, x), ex_of(h, l, (x + d) % X)) for h, l, x in coords]

    def shift_c(d):
        return [(y * L + c, y * L + (c + d) % L) for y in range(H) for c in range(L)]

    def shift_y(d):
        return [(y * L + c, (y + d) % H * L + c) for y in range(H) for c in range(L)]

    def home(t, s):
        pairs = []
        for h, l, x in coords:
            for y in range(H):
                k = (y - h) % H
                dh, dx = (t + k) % H, k * Q + s
                for c in range(L):
                    src = ex_of(h, l, x) * F + y * L + c
                    dst = ex_of((h - dh) % H, l, (x - dx) % X) * F + h * L + c
                    pairs.append((src, dst))
        return pairs

    def mod(v, n):
        return lax.rem(v + 4 * n, n)

    def pick(options, index):
        out = options[0]
        for i in range(1, len(options)):
            out = jnp.where(index == i, options[i], out)
        return out

    def dot(a, b):
        return jnp.dot(a, b, preferred_element_type=jnp.float32)

    def local(a, b, test, weights):
        rows, cols = a.shape[0], b.shape[1]
        e, f = lax.axis_index("ex"), lax.axis_index("feat")
        h, l, x = lax.div(e, L * X), lax.rem(lax.div(e, X), L), lax.rem(e, X)
        y, c = lax.div(f, L), lax.rem(f, L)
        k = mod(y - h, H)

        r_cuts = [0, rows // 2, rows // 2 + rows // 3, rows]
        n_r = len(r_cuts) - 1
        if cols % 512 == 0:
            w, c_cuts = cols // 4, [0, 2, 3, 4]
        else:
            w, c_cuts = cols, [0, 1]
        n_c = len(c_cuts) - 1
        n_g = c_cuts[-1]

        def rows_of(v, i):
            return v[r_cuts[i] : r_cuts[i + 1]]

        a_in = [rows_of(a, i) for i in range(n_r)]
        b_in = [b[:, c_cuts[j] * w : c_cuts[j + 1] * w] for j in range(n_c)]
        far = [[lax.ppermute(p, "ex", shift_h(dh)) for p in a_in] for dh in range(1, H)]
        b_l = [[lax.ppermute(p, "ex", shift_l(dl)) for p in b_in] for dl in range(1, L)]
        near = [a] + [lax.ppermute(a, "ex", shift_x(dx)) for dx in range(1, X)]
        far_x = [
            [pieces]
            + [[lax.ppermute(p, "ex", shift_x(dx)) for p in pieces] for dx in range(1, X)]
            for pieces in far
        ]

        late, _ = lax.optimization_barrier((test, far[-1][-1] if far else test))
        tests = late
        for axis_shift, n in ((shift_h, H), (shift_l, L), (shift_x, X)):
            tests = jnp.stack(
                [tests] + [lax.ppermute(tests, "ex", axis_shift(d)) for d in range(1, n)]
            )
        tests = jnp.transpose(tests, (2, 1, 0, 3, 4))
        tests = tests.reshape(-1, tests.shape[-1])

        products = {}

        def product(dh, dx, dl, i, g):
            j = None if dl == 0 else next(n for n in range(n_c) if g < c_cuts[n + 1])
            piece = None if dh == 0 else i
            key = dh, dx, dl, piece, j
            if key not in products:
                lhs = near[dx] if dh == 0 else far_x[dh - 1][dx][i]
                products[key] = dot(lhs, b if dl == 0 else b_l[dl - 1][j])
            out = products[key]
            out = rows_of(out, i) if dh == 0 else out
            g = g if dl == 0 else g - c_cuts[j]
            return out[:, g * w : (g + 1) * w]

        got = {}
        gate = []

        def unit(blocks):
            n = sum(r_cuts[i + 1] - r_cuts[i] for i, g in blocks)

            taken = [
                [product(dh, dx, dl, i, g) for dl in range(L)]
                for dh in range(H)
                for dx in range(X)
                for i, g in blocks
            ]
            if gate:
                taken, _ = lax.optimization_barrier((taken, gate[-1]))

            def stack(d):
                return jnp.concatenate([pick(v, mod(l - c - d, L)) for v in taken], axis=0)

            sends = [stack(d) for d in range(1, L)]
            gate.append(sends)
            sent = [lax.ppermute(v, "feat", shift_c(d + 1)) for d, v in enumerate(sends)]
            total = stack(0)
            for s in sent:
                total = total + s
            total = total.reshape(H, H, Q * n, w)
            kept = pick([total[:, i] for i in range(H)], k)
            for d in range(1, H):
                out = pick([total[:, i] for i in range(H)], mod(k + d, H)).astype(jnp.bfloat16)
                kept = kept + lax.ppermute(out, "feat", shift_y(d)).astype(jnp.float32)
            final = kept.astype(jnp.bfloat16)
            for t in range(H):
                out = pick([final[i] for i in range(H)], mod(t + k, H))
                for s in range(Q):
                    res = lax.ppermute(out[s * n : (s + 1) * n], both, home(t, s))
                    r = 0
                    for i, g in blocks:
                        m = r_cuts[i + 1] - r_cuts[i]
                        got[t * Q + s, i, g] = res[r : r + m]
                        r += m

        done = []
        for j in range(n_c):
            for i in range(n_r):
                for g in range(c_cuts[j], c_cuts[j + 1]):
                    done.append((max(i, j * (n_r - 1) // max(n_c - 1, 1)), i, g))
        for stage in range(n_r):
            blocks = [(i, g) for s, i, g in done if s == stage]
            if blocks:
                unit(blocks)

        slots = [
            jnp.concatenate(
                [
                    jnp.concatenate([got[n, i, g] for g in range(n_g)], axis=1)
                    for i in range(n_r)
                ],
                axis=0,
            )
            for n in range(X)
        ]
        projected = []
        for kx in range(X):
            dx = mod(kx - x, X)
            t = mod(y - h - lax.div(dx, Q), H)
            projected.append(pick(slots, t * Q + lax.rem(dx, Q)))
        projected = jnp.concatenate(projected, axis=1)

        part = lax.dot_general(
            tests, projected, (((1,), (1,)), ((), ())), preferred_element_type=jnp.float32
        )
        part = part.reshape(H, L, part.shape[0] // F, part.shape[1])
        mine = pick([part[:, d] for d in range(L)], mod(l - c, L))
        for d in range(1, L):
            out = pick([part[:, i] for i in range(L)], mod(l - c - d, L))
            mine = mine + lax.ppermute(out, "feat", shift_c(d))
        inner = pick([mine[d] for d in range(H)], mod(h - y, H))
        for d in range(1, H):
            out = pick([mine[i] for i in range(H)], mod(h - y - d, H))
            inner = inner + lax.ppermute(out, "feat", shift_y(d))
        own = inner.shape[0] // X
        inner = jnp.concatenate(
            [
                pick([inner[d * own : (d + 1) * own] for d in range(X)], mod(x - kx, X))
                for kx in range(X)
            ],
            axis=0,
        )
        return inner * weights[None, :], projected

    return jax.shard_map(
        local,
        mesh=mesh,
        in_specs=(P("ex", "feat"), P("feat", "ex"), P("ex", "feat"), P("ex")),
        out_specs=(P("feat", "ex"), P("ex", "feat")),
        check_vma=False,
    )
```
